32 devices in a mesh: section: 2 (over x), wrow: 4 (over y, core), wcol: 4 (over z).
Axes of the slice: x: 2, y: 2, z: 4, core: 2. Of those that a mesh axis runs over, the one named last changes fastest.
Arguments:
- states: bfloat16 [2, 64, 64, 1536], P(None, 'wrow', 'wcol'), may hold values from -6 to 6
- timesteps: int32 [2], replicated, may hold values from 0 to 999, as said below
- shifts: int32 [2, 2], P('section'), may hold values from 1 to 4
- qkv_weight: bfloat16 [2, 1536, 2304], P('section', None, 'wcol'), may hold values from -0.15625 to 0.15625
- out_weight: bfloat16 [2, 768, 1536], P('section', None, 'wcol'), may hold values from -0.21875 to 0.21875
- mod_weight: bfloat16 [2, 256, 4608], P('section', None, 'wcol'), may hold values from -0.375 to 0.375
Outputs:
- layer_states: bfloat16 [2, 2, 64, 64, 1536], P('section', None, 'wrow', 'wcol')
The draws below stay inside these ranges and needn't reach their ends.
Inputs may be any that keep to these rules, and one draw needn't show every extreme that they name: The 2 timesteps are distinct.
All inputs are finite; a program needn't handle non-finite values.
Results may differ from the reference program's by a relative error of at most 0.0053.
Values may be sent and summed in bfloat16 or wider, within the bound.
No kernel may reach another device: no remote copies, remote signals or barrier semaphores. Data moves between devices by JAX's collectives and lax.ppermute only.
A program may use at most 128 MiB of HBM per device.

```python
import math
import jax
import jax.numpy as jnp
from jax import lax

D = 1536
HEADS = 6
HD = 128
TEMB = 256
WIN = 8
MB = 2
HH = 768
QKV = 2304
NH = 64
NW = 64
SECTIONS = 2
N_SECTION = 2


def draw_timesteps(key, part):
    first_key, second_key = jax.random.split(jax.random.fold_in(key, 7129))
    largest_step = 999 // max(MB - 1, 1)
    step_value = jax.random.randint(first_key, (), 1, largest_step + 1, dtype=jnp.int32)
    counter = jnp.arange(MB, dtype=jnp.int32)
    values = 999 - counter * step_value
    offset = jax.random.randint(second_key, (), 0, MB, dtype=jnp.int32)
    return jnp.roll(values, offset).astype(jnp.int32)


def plant(values, key, least, top_value):
    longest = values.shape.index(max(values.shape))
    spots = []
    for shift in (0, 1):
        where = [jax.random.randint(jax.random.fold_in(key, axis), (), 0, length) for axis, length in enumerate(values.shape)]
        where[longest] = (where[longest] + shift) % values.shape[longest]
        spots.append(tuple(where))
    return values.at[spots[0]].set(least).at[spots[1]].set(top_value)


def steps_of(key, extent, pieces, smallest, largest):
    gain, own = 1.0, jax.random.fold_in(key, 6)
    for position, blocks in pieces:
        steps = jnp.exp(jax.random.uniform(jax.random.fold_in(own, position), (blocks,), jnp.float32, smallest / len(pieces), largest / len(pieces)))
        gain = gain * jnp.repeat(steps, extent[position] // blocks).reshape([-1 if axis == position else 1 for axis in range(len(extent))])
    return gain


def normal_values(stream_key, dims, width, most, shards=(), held_as=jnp.bfloat16):
    values = width * jax.random.normal(stream_key, dims, jnp.float32)
    if shards:
        values = values * steps_of(stream_key, dims, shards, -0.22, 0.18)
    return jnp.clip(values, -most, most).astype(held_as)


def setup_inputs(seed: int = 0) -> dict:
    key_list = jax.random.split(jax.random.key(seed), 7)
    states = normal_values(key_list[0], (MB, NH, NW, D), 1.0, 6.0, ((1, 4), (2, 4)))
    timesteps = draw_timesteps(jax.random.fold_in(key_list[6], 71), 0)
    shifts = plant(jax.random.randint(key_list[2], (SECTIONS, 2), 1, WIN // 2 + 1), jax.random.fold_in(key_list[2], 1), 1, (WIN // 2 + 1) - 1).astype(jnp.int32)
    qkv_weight = normal_values(key_list[3], (SECTIONS, D, QKV), D ** -0.5, 0.15625, ((0, 2), (2, 4)))
    out_weight = normal_values(key_list[4], (SECTIONS, HH, D), HH ** -0.5, 0.21875, ((0, 2), (2, 4)))
    mod_weight = normal_values(key_list[5], (SECTIONS, TEMB, 3 * D), TEMB ** -0.5, 0.375, ((0, 2), (2, 4)))
    return dict(states=states, timesteps=timesteps, shifts=shifts, qkv_weight=qkv_weight, out_weight=out_weight, mod_weight=mod_weight)


epsilon = 1e-06

def sinusoid(moments, entries):
    half_count = entries // 2
    frequency = jnp.exp(-math.log(10000.0) * jnp.arange(half_count, dtype=jnp.float32) / half_count)
    angles = moments.astype(jnp.float32)[:, None] * frequency[None, :]
    return jnp.concatenate([jnp.cos(angles), jnp.sin(angles)], axis=1)

def rounded(number):
    return lax.optimization_barrier(number.astype(jnp.bfloat16)).astype(jnp.float32)

def layer_norm(region):
    values = region.astype(jnp.float32)
    center = values - lax.optimization_barrier(jnp.mean(values, axis=-1, keepdims=True))
    spread = lax.optimization_barrier(jnp.mean(center * center, axis=-1, keepdims=True))
    return center * lax.rsqrt(spread + epsilon)

def window_attention(triples):
    tile_rows, tile_cols, feature_width = triples.shape
    windowed = triples.reshape(tile_rows // WIN, WIN, tile_cols // WIN, WIN, 3, HEADS, HD)
    windowed = windowed.transpose(4, 0, 2, 5, 1, 3, 6).reshape(3, tile_rows // WIN * (tile_cols // WIN), HEADS, WIN * WIN, HD)
    scores = jnp.einsum('nhqd,nhkd->nhqk', windowed[0].astype(jnp.float32), windowed[1].astype(jnp.float32)) * HD ** (-0.5)
    weights = jnp.exp(scores)
    probabilities = (weights / lax.optimization_barrier(jnp.sum(weights, axis=-1, keepdims=True))).astype(jnp.bfloat16)
    attended = jnp.einsum('nhqk,nhkd->nhqd', probabilities.astype(jnp.float32), windowed[2].astype(jnp.float32)).astype(jnp.bfloat16)
    attended = attended.reshape(tile_rows // WIN, tile_cols // WIN, HEADS, WIN, WIN, HD).transpose(0, 3, 1, 4, 2, 5)
    return attended.reshape(tile_rows, tile_cols, HEADS * HD)

def by_bands(function, *arrays):
    stacked = tuple((member.reshape((member.shape[0] // WIN, WIN) + member.shape[1:]) for member in arrays))
    result = lax.map(lambda members: function(*members), stacked)
    return result.reshape((-1,) + result.shape[2:])

def shifted_layer(inputs, modulation, shift_pair, qkv_matrix, out_matrix):
    mod_shift = modulation[:D]
    mod_scale = modulation[D:2 * D]
    mod_gate = modulation[2 * D:]

    def normalize(stripe):
        return (layer_norm(stripe) * (1.0 + mod_scale) + mod_shift).astype(jnp.bfloat16)
    normed = by_bands(normalize, inputs)
    rolled = jnp.roll(normed, (-shift_pair[0], -shift_pair[1]), axis=(0, 1))

    def attend(stripe):
        tile_rows, tile_cols, feature_width = stripe.shape
        triples = jnp.dot(stripe.reshape(tile_rows * tile_cols, feature_width), qkv_matrix, preferred_element_type=jnp.float32)
        return window_attention(triples.astype(jnp.bfloat16).reshape(tile_rows, tile_cols, -1))
    attended = by_bands(attend, rolled)
    restored = jnp.roll(attended, (shift_pair[0], shift_pair[1]), axis=(0, 1))

    def finish(stripe, residual):
        tile_rows, tile_cols, feature_width = stripe.shape
        projection = jnp.dot(stripe.reshape(tile_rows * tile_cols, feature_width), out_matrix, preferred_element_type=jnp.float32)
        projection = rounded(projection).reshape(tile_rows, tile_cols, -1)
        return (residual.astype(jnp.float32) + mod_gate * projection).astype(jnp.bfloat16)
    return by_bands(finish, restored, inputs)

def reference(states, timesteps, shifts, qkv_weight, out_weight, mod_weight):
    embedding = jax.nn.silu(sinusoid(timesteps, TEMB)).astype(jnp.bfloat16)
    current = states
    results = []
    for section_index in range(N_SECTION):
        modulations = rounded(jnp.dot(embedding, mod_weight[section_index], preferred_element_type=jnp.float32))
        current = jnp.stack([shifted_layer(current[member], modulations[member], shifts[section_index], qkv_weight[section_index], out_weight[section_index]) for member in range(MB)])
        results.append(current)
    return jnp.stack(results)
```

```python
import functools
import math

import jax
import jax.numpy as jnp
from jax import lax
from jax.experimental import pallas as pl
from jax.experimental.pallas import tpu as pltpu
from jax.sharding import PartitionSpec as P

HEADS = 6
HD = 128
TEMB = 256
WIN = 8
MB = 2
MARGIN = WIN // 2

epsilon = 1e-06


def ring(value, axis, by):
    devices = lax.axis_size(axis)
    return lax.ppermute(value, axis, [(i, (i + by) % devices) for i in range(devices)])


def swap(value, axis, bit):
    devices = lax.axis_size(axis)
    return lax.ppermute(value, axis, [(i, i ^ bit) for i in range(devices)])


def sinusoid(moments, entries):
    half_count = entries // 2
    frequency = jnp.exp(-math.log(10000.0) * jnp.arange(half_count, dtype=jnp.float32) / half_count)
    angles = moments.astype(jnp.float32)[:, None] * frequency[None, :]
    return jnp.concatenate([jnp.cos(angles), jnp.sin(angles)], axis=1)


def attend_kernel(columns, cols, x_ref, shift_ref, scale_ref, w_ref, out_ref, normed, triples):
    step = pl.program_id(0)
    blocks = pl.num_programs(0)
    piece = w_ref.shape[2]

    @pl.when(step == 0)
    def _():
        values = x_ref[...].astype(jnp.float32)
        center = values - jnp.mean(values, axis=-1, keepdims=True)
        spread = jnp.mean(center * center, axis=-1, keepdims=True)
        scaled = center * lax.rsqrt(spread + epsilon)
        normed[...] = (scaled * (1.0 + scale_ref[...]) + shift_ref[...]).astype(normed.dtype)

    product = jnp.dot(normed[...], w_ref[0], preferred_element_type=jnp.float32)
    product = product.astype(triples.dtype)
    for block in range(columns // piece):

        @pl.when(step == block)
        def _(block=block):
            triples[:, block * piece : (block + 1) * piece] = product

    @pl.when(step == blocks - 1)
    def _():
        tokens = x_ref.shape[0]
        width = columns // 3
        band = WIN * cols
        side = lax.broadcasted_iota(jnp.int32, (band, band), 0) % cols // WIN
        other = lax.broadcasted_iota(jnp.int32, (band, band), 1) % cols // WIN
        same = side == other
        for start in range(0, tokens, band):
            for head in range(width // HD):
                rows = slice(start, start + band)
                q = triples[rows, head * HD : (head + 1) * HD]
                k = triples[rows, width + head * HD : width + (head + 1) * HD]
                v = triples[rows, 2 * width + head * HD : 2 * width + (head + 1) * HD]
                scores = lax.dot_general(
                    q, k, (((1,), (1,)), ((), ())), preferred_element_type=jnp.float32
                )
                weights = jnp.where(same, jnp.exp(scores * HD ** (-0.5)), 0.0)
                total = jnp.sum(weights, axis=-1, keepdims=True)
                probabilities = (weights / total).astype(v.dtype)
                attended = jnp.dot(probabilities, v, preferred_element_type=jnp.float32)
                out_ref[rows, head * HD : (head + 1) * HD] = attended.astype(out_ref.dtype)


def attend(x, shift, scale, weight):
    rows, cols, width = x.shape
    blocks, depth, piece = weight.shape
    columns = blocks * piece
    tokens = rows * cols
    out = pl.pallas_call(
        functools.partial(attend_kernel, columns, cols),
        grid=(blocks,),
        in_specs=[
            pl.BlockSpec((tokens, width), lambda i: (0, 0)),
            pl.BlockSpec((1, width), lambda i: (0, 0)),
            pl.BlockSpec((1, width), lambda i: (0, 0)),
            pl.BlockSpec((1, depth, piece), lambda i: (i, 0, 0)),
        ],
        out_specs=pl.BlockSpec((tokens, columns // 3), lambda i: (0, 0)),
        out_shape=jax.ShapeDtypeStruct((tokens, columns // 3), jnp.bfloat16),
        scratch_shapes=[
            pltpu.VMEM((tokens, width), jnp.bfloat16),
            pltpu.VMEM((tokens, columns), jnp.bfloat16),
        ],
        cost_estimate=pl.CostEstimate(
            flops=2 * tokens * width * columns,
            bytes_accessed=2 * (width * columns + tokens * width + tokens * columns // 3),
            transcendentals=tokens * WIN * cols * HEADS,
        ),
        name="attend",
    )(x.reshape(tokens, width), shift[None], scale[None], weight)
    return out.reshape(rows, cols, columns // 3)


def finish_kernel(att_ref, w_ref, x_ref, gate_ref, out_ref):
    step = pl.program_id(0)
    piece = w_ref.shape[2]
    projection = jnp.dot(att_ref[...], w_ref[0], preferred_element_type=jnp.float32)
    projection = projection.astype(jnp.bfloat16).astype(jnp.float32)
    for block in range(x_ref.shape[1] // piece):
        part = slice(block * piece, (block + 1) * piece)

        @pl.when(step == block)
        def _(part=part):
            residual = x_ref[:, part].astype(jnp.float32)
            out_ref[:, part] = (residual + gate_ref[:, part] * projection).astype(out_ref.dtype)


def finish(attended, weight, x, gate):
    rows, cols, width = x.shape
    blocks, depth, piece = weight.shape
    tokens = rows * cols
    out = pl.pallas_call(
        finish_kernel,
        grid=(blocks,),
        in_specs=[
            pl.BlockSpec((tokens, depth), lambda i: (0, 0)),
            pl.BlockSpec((1, depth, piece), lambda i: (i, 0, 0)),
            pl.BlockSpec((tokens, width), lambda i: (0, 0)),
            pl.BlockSpec((1, width), lambda i: (0, 0)),
        ],
        out_specs=pl.BlockSpec((tokens, width), lambda i: (0, 0)),
        out_shape=jax.ShapeDtypeStruct((tokens, width), jnp.bfloat16),
        cost_estimate=pl.CostEstimate(
            flops=2 * tokens * width * depth,
            bytes_accessed=2 * (width * depth + 2 * tokens * width + tokens * depth),
            transcendentals=0,
        ),
        name="finish",
    )(attended.reshape(tokens, depth), weight, x.reshape(tokens, width), gate[None])
    return out.reshape(rows, cols, width)


def along_z(piece):
    return [piece] + [ring(piece, "wcol", by) for by in range(1, lax.axis_size("wcol"))]


def own_rows(matrix):
    across = lax.axis_size("wrow")
    rows = matrix.shape[0] // across
    return lax.dynamic_slice_in_dim(matrix, lax.axis_index("wrow") * rows, rows, 0)


def across_rows(pieces):
    across = lax.axis_size("wrow")
    held = [{0: piece} for piece in pieces]
    bit = across // 2
    while bit:
        for parts in held:
            known = sorted(parts)
            sent = jnp.stack([parts[k] for k in known]) if len(known) > 1 else parts[0][None]
            got = swap(sent, "wrow", bit)
            for place, k in enumerate(known):
                parts[k ^ bit] = got[place]
        bit //= 2
    return held


def assemble(held):
    along, across = lax.axis_size("wcol"), lax.axis_size("wrow")
    rows, columns = held[0][0].shape
    full = jnp.zeros((along, across, rows, columns), held[0][0].dtype)
    row, col = lax.axis_index("wrow"), lax.axis_index("wcol")
    for by, parts in enumerate(held):
        for k, part in parts.items():
            place = ((col - by) % along, row ^ k, 0, 0)
            full = lax.dynamic_update_slice(full, part[None, None], place)
    return full.reshape(along, across * rows, columns)


def gather_vectors(part):
    along = lax.axis_size("wcol")
    col = lax.axis_index("wcol")
    members, width = part.shape
    full = jnp.zeros((along, members, width), part.dtype)
    for by, piece in enumerate(along_z(part)):
        full = lax.dynamic_update_slice(full, piece[None], ((col - by) % along, 0, 0))
    return full.transpose(1, 0, 2).reshape(members, along * width)


def widen(block, before, after, axis, name):
    parts = [block]
    size = block.shape[axis]
    if before:
        border = lax.slice_in_dim(block, size - before, size, axis=axis)
        parts.insert(0, ring(border, name, 1))
    if after:
        parts.append(ring(lax.slice_in_dim(block, 0, after, axis=axis), name, -1))
    return jnp.concatenate(parts, axis=axis)


def window_of(block, row, col, rows, cols):
    block = lax.dynamic_slice_in_dim(block, row, rows, block.ndim - 3)
    return lax.dynamic_slice_in_dim(block, col, cols, block.ndim - 2)


def per_device(states, timesteps, shifts, qkv_weight, out_weight, mod_weight):
    section = lax.axis_index("section")
    first = section == 0
    members, rows, cols, width = states.shape

    qkv_pieces = along_z(own_rows(qkv_weight[0]))

    embedding = jax.nn.silu(sinusoid(timesteps, TEMB)).astype(jnp.bfloat16)
    mod_part = jnp.dot(embedding, mod_weight[0], preferred_element_type=jnp.float32).astype(
        jnp.bfloat16
    )
    mods = gather_vectors(mod_part)
    mods_other = swap(mods, "section", 1)
    shifts_other = swap(shifts[0], "section", 1)
    mods_first = jnp.where(first, mods, mods_other).astype(jnp.float32)
    mods = mods.astype(jnp.float32)
    here = shifts[0]
    begin = jnp.where(first, here, shifts_other)

    wide = widen(states, 0, MARGIN, 1, "wrow")
    wide = lax.dynamic_slice_in_dim(wide, here[0], rows, 1)
    wide = widen(wide, 0, MARGIN, 2, "wcol")
    rolled = lax.dynamic_slice_in_dim(wide, here[1], cols, 2)

    qkv_full = assemble(across_rows(qkv_pieces))

    out_pieces = along_z(own_rows(out_weight[0]))
    out_stack = jnp.stack(out_pieces)
    out_other = swap(out_stack, "section", 1)
    out_begin = jnp.where(first, out_stack, out_other)
    along = lax.axis_size("wcol")
    begin_full = assemble(across_rows([out_begin[j] for j in range(along)]))
    own_full = assemble(across_rows(out_pieces))

    results = []
    for member in range(members):
        attended = attend(
            rolled[member], mods[member, :width], mods[member, width : 2 * width], qkv_full
        )
        other = swap(attended, "section", 1)
        attended = jnp.where(first, attended, other)
        attended = widen(attended, MARGIN, MARGIN, 0, "wrow")
        attended = widen(attended, MARGIN, MARGIN, 1, "wcol")
        plain = window_of(attended, MARGIN - begin[0], MARGIN - begin[1], rows, cols)
        turned = window_of(
            attended,
            MARGIN - begin[0] + here[0],
            MARGIN - begin[1] + here[1],
            rows,
            cols,
        )
        gate_first = mods_first[member, 2 * width :]
        inner = finish(turned, begin_full, rolled[member], gate_first)
        state = finish(plain, begin_full, states[member], gate_first)
        attended = attend(
            inner, mods[member, :width], mods[member, width : 2 * width], qkv_full
        )
        attended = widen(attended, MARGIN, 0, 0, "wrow")
        attended = widen(attended, MARGIN, 0, 1, "wcol")
        attended = window_of(attended, MARGIN - here[0], MARGIN - here[1], rows, cols)
        last = finish(attended, own_full, state, mods[member, 2 * width :])
        results.append(jnp.where(first, state, last))
    return jnp.stack(results)[None]


def solution(mesh):
    in_specs = (
        P(None, "wrow", "wcol", None),
        P(),
        P("section", None),
        P("section", None, "wcol"),
        P("section", None, "wcol"),
        P("section", None, "wcol"),
    )
    out_specs = P("section", None, "wrow", "wcol", None)
    return jax.shard_map(
        per_device, mesh=mesh, in_specs=in_specs, out_specs=out_specs, check_vma=False
    )
```

```python
import functools
import math

import jax
import jax.numpy as jnp
from jax import lax
from jax.experimental import pallas as pl
from jax.experimental.pallas import tpu as pltpu
from jax.sharding import PartitionSpec as P

HEADS = 6
HD = 128
TEMB = 256
WIN = 8
MB = 2
MARGIN = WIN // 2

epsilon = 1e-06


VMEM_BLOCK = pl.BlockSpec(memory_space=pltpu.VMEM)
ANY_BLOCK = pl.BlockSpec(memory_space=pl.ANY)
SMEM_BLOCK = pl.BlockSpec(memory_space=pltpu.SMEM)


def ring(value, axis, by):
    devices = lax.axis_size(axis)
    return lax.ppermute(value, axis, [(i, (i + by) % devices) for i in range(devices)])


def swap(value, axis, bit):
    devices = lax.axis_size(axis)
    return lax.ppermute(value, axis, [(i, i ^ bit) for i in range(devices)])


def passed(value, down, right):
    across, along = lax.axis_size("wrow"), lax.axis_size("wcol")
    pairs = []
    for row in range(across):
        for col in range(along):
            target = (row + down) % across * along + (col + right) % along
            pairs.append((row * along + col, target))
    return lax.ppermute(value, ("wrow", "wcol"), pairs)


def sinusoid(moments, entries):
    half_count = entries // 2
    frequency = jnp.exp(-math.log(10000.0) * jnp.arange(half_count, dtype=jnp.float32) / half_count)
    angles = moments.astype(jnp.float32)[:, None] * frequency[None, :]
    return jnp.concatenate([jnp.cos(angles), jnp.sin(angles)], axis=1)


def copies_of(parts, refs, held, sems, row, col):
    blocks, depth, _ = held.shape
    jobs = []
    for number, (slot, index, by, k) in enumerate(parts):
        source = refs[slot] if index is None else refs[slot].at[index]
        block = lax.rem(col - by + blocks, blocks) if blocks > 1 else 0
        target = held.at[block]
        if k is not None:
            rows = source.shape[0]
            start = pl.multiple_of(lax.bitwise_xor(row, k) * rows, 16)
            target = target.at[pl.ds(start, rows)]
        jobs.append((by, pltpu.make_async_copy(source, target, sems.at[number])))
    return jobs


def layout_of(parts):
    arrays, layout = [], []
    for array, index, by, k in parts:
        slot = next((i for i, a in enumerate(arrays) if a is array), None)
        if slot is None:
            slot = len(arrays)
            arrays.append(array)
        layout.append((slot, index, by, k))
    return arrays, layout


def choose(rows, cols, wanted):
    sizes = []
    for down, right in wanted:
        sizes.append((MARGIN if down else rows, MARGIN if right else cols))
    tokens = rows * cols
    matrices = []
    for (down, right), (high, wide) in zip(wanted, sizes):
        cell = lax.broadcasted_iota(jnp.int32, (high * wide, 1), 0)
        i, j = cell // wide, cell % wide
        i = i + (rows - MARGIN if down > 0 else 0)
        j = j + (cols - MARGIN if right > 0 else 0)
        lane = lax.broadcasted_iota(jnp.int32, (high * wide, tokens), 1)
        matrices.append((lane == i * cols + j).astype(jnp.float32).astype(jnp.bfloat16))
    return matrices


def border_shape(rows, cols, down, right):
    return (MARGIN if down else rows) * (MARGIN if right else cols)


def attend_kernel(count, layout, rows, cols, wanted, *refs):
    place, normed = refs[0], refs[1]
    parts = refs[2 : 2 + count]
    out = refs[2 + count]
    borders = refs[3 + count : 3 + count + len(wanted)]
    held, triples, sems = refs[3 + count + len(wanted) :]
    blocks, _, piece = held.shape
    width = blocks * piece // 3
    row, col = place[0], place[1]
    jobs = copies_of(layout, parts, held, sems, row, col)
    for _, job in jobs:
        job.start()
    for by in range(blocks):
        for where, job in jobs:
            if where == by:
                job.wait()
        block = lax.rem(col - by + blocks, blocks) if blocks > 1 else 0
        product = jnp.dot(normed[...], held[block], preferred_element_type=jnp.float32)
        triples[block] = product.astype(triples.dtype)

    def columns(band, start):
        got = []
        stop = start + HD
        while start < stop:
            block, inner = divmod(start, piece)
            length = min(stop - start, piece - inner)
            got.append(triples[block, band, inner : inner + length])
            start += length
        return got[0] if len(got) == 1 else jnp.concatenate(got, axis=1)

    size = WIN * cols
    side = lax.broadcasted_iota(jnp.int32, (size, size), 0) % cols // WIN
    other = lax.broadcasted_iota(jnp.int32, (size, size), 1) % cols // WIN
    same = side == other
    heads = width // HD
    for start in range(0, rows * cols, size):
        band = slice(start, start + size)
        scores = []
        for head in range(heads):
            q = columns(band, head * HD)
            k = columns(band, width + head * HD)
            scores.append(
                lax.dot_general(q, k, (((1,), (1,)), ((), ())), preferred_element_type=jnp.float32)
            )
        probabilities = []
        for score in scores:
            weights = jnp.where(same, jnp.exp(score * HD ** (-0.5)), 0.0)
            total = jnp.sum(weights, axis=-1, keepdims=True)
            probabilities.append((weights * (1.0 / total)).astype(jnp.bfloat16))
        for head in range(heads):
            v = columns(band, 2 * width + head * HD)
            attended = jnp.dot(probabilities[head], v, preferred_element_type=jnp.float32)
            out[band, head * HD : (head + 1) * HD] = attended.astype(out.dtype)
    for matrix, ref in zip(choose(rows, cols, wanted), borders):
        ref[...] = jnp.dot(matrix, out[...], preferred_element_type=jnp.float32).astype(ref.dtype)


def attend(place, normed, parts, blocks, rows, cols, wanted):
    tokens, width = normed.shape
    arrays, layout = layout_of(parts)
    piece = arrays[0].shape[-1]
    columns = blocks * piece
    inner = columns // 3
    shapes = [jax.ShapeDtypeStruct((tokens, inner), jnp.bfloat16)]
    for down, right in wanted:
        shapes.append(
            jax.ShapeDtypeStruct((border_shape(rows, cols, down, right), inner), jnp.bfloat16)
        )
    return pl.pallas_call(
        functools.partial(attend_kernel, len(arrays), layout, rows, cols, wanted),
        in_specs=[SMEM_BLOCK, VMEM_BLOCK] + [ANY_BLOCK] * len(arrays),
        out_specs=[VMEM_BLOCK] * len(shapes),
        out_shape=shapes,
        scratch_shapes=[
            pltpu.VMEM((blocks, width, piece), jnp.bfloat16),
            pltpu.VMEM((blocks, tokens, piece), jnp.bfloat16),
            pltpu.SemaphoreType.DMA((len(layout),)),
        ],
        cost_estimate=pl.CostEstimate(
            flops=2 * tokens * width * columns,
            bytes_accessed=2 * (width * columns + tokens * width + tokens * inner),
            transcendentals=tokens * WIN * cols * HEADS,
        ),
        compiler_params=pltpu.CompilerParams(vmem_limit_bytes=32 * 1024 * 1024),
        name="attend",
    )(place, normed, *arrays)


def border_kernel(rows, cols, wanted, place, mine, theirs, out, *borders):
    @pl.when(place[2] == 0)
    def _():
        out[...] = mine[...]

    @pl.when(place[2] != 0)
    def _():
        out[...] = theirs[...]

    for matrix, ref in zip(choose(rows, cols, wanted), borders):
        ref[...] = jnp.dot(matrix, out[...], preferred_element_type=jnp.float32).astype(ref.dtype)


def borders_of(place, mine, theirs, rows, cols, wanted):
    inner = mine.shape[-1]
    shapes = [jax.ShapeDtypeStruct(mine.shape, mine.dtype)]
    for down, right in wanted:
        shapes.append(
            jax.ShapeDtypeStruct((border_shape(rows, cols, down, right), inner), mine.dtype)
        )
    return pl.pallas_call(
        functools.partial(border_kernel, rows, cols, wanted),
        in_specs=[SMEM_BLOCK, VMEM_BLOCK, VMEM_BLOCK],
        out_specs=[VMEM_BLOCK] * len(shapes),
        out_shape=shapes,
        cost_estimate=pl.CostEstimate(
            flops=2 * mine.shape[0] * inner * 320, bytes_accessed=8 * mine.size, transcendentals=0
        ),
        name="borders",
    )(place, mine, theirs)


def finish_kernel(count, layout, rows, cols, wanted, shifts, kind, *refs):
    place, vectors, inputs, main = refs[:4]
    borders = refs[4 : 4 + len(wanted)]
    parts = refs[4 + len(wanted) : 4 + len(wanted) + count]
    out, held, extended, moved, result, sems = refs[4 + len(wanted) + count :]
    blocks, depth, piece = held.shape
    row, col = place[0], place[1]
    jobs = copies_of(layout, parts, held, sems, row, col)
    for _, job in jobs:
        job.start()

    tokens = rows * cols
    extended[0:tokens] = main[...]
    down, right = place[shifts[0]], place[shifts[1]]
    cell = lax.broadcasted_iota(jnp.int32, (tokens, 1), 0)
    i, j = cell // cols + down, cell % cols + right
    source = i * cols + j
    offset = tokens
    for (dr, dc), ref in zip(wanted, borders):
        size = ref.shape[0]
        extended[offset : offset + size] = ref[...]
        wide = MARGIN if dc else cols
        top = {1: -MARGIN, 0: 0, -1: rows}[dr]
        left = {1: -MARGIN, 0: 0, -1: cols}[dc]
        inside = {1: i < 0, 0: (i >= 0) & (i < rows), -1: i >= rows}[dr]
        inside &= {1: j < 0, 0: (j >= 0) & (j < cols), -1: j >= cols}[dc]
        source = jnp.where(inside, offset + (i - top) * wide + (j - left), source)
        offset += size
    lane = lax.broadcasted_iota(jnp.int32, (tokens, offset), 1)
    matrix = (lane == source).astype(jnp.float32).astype(jnp.bfloat16)
    moved[...] = jnp.dot(matrix, extended[...], preferred_element_type=jnp.float32).astype(
        moved.dtype
    )
    for _, job in jobs:
        job.wait()
    for block in range(blocks):
        part = slice(block * piece, (block + 1) * piece)
        projection = jnp.dot(moved[...], held[block], preferred_element_type=jnp.float32)
        projection = projection.astype(jnp.bfloat16).astype(jnp.float32)
        state = inputs[:, part].astype(jnp.float32) + vectors[0:1, part] * projection
        result[:, part] = state.astype(result.dtype)
    if kind == "norm":
        values = result[...].astype(jnp.float32)
        center = values - jnp.mean(values, axis=-1, keepdims=True)
        spread = jnp.mean(center * center, axis=-1, keepdims=True)
        scaled = center * lax.rsqrt(spread + epsilon)
        out[...] = (scaled * (1.0 + vectors[1:2, :]) + vectors[2:3, :]).astype(out.dtype)
    elif kind == "last":
        out[...] = jnp.where(place[2] == 0, inputs[...], result[...])
    else:
        out[...] = result[...]


def finish(place, vectors, inputs, main, borders, parts, blocks, rows, cols, wanted, shifts, kind):
    tokens, width = inputs.shape
    depth = main.shape[-1]
    arrays, layout = layout_of(parts)
    piece = arrays[0].shape[-1]
    total = tokens + sum(border_shape(rows, cols, *w) for w in wanted)
    return pl.pallas_call(
        functools.partial(finish_kernel, len(arrays), layout, rows, cols, wanted, shifts, kind),
        in_specs=[SMEM_BLOCK] + [VMEM_BLOCK] * (3 + len(wanted)) + [ANY_BLOCK] * len(arrays),
        out_specs=VMEM_BLOCK,
        out_shape=jax.ShapeDtypeStruct((tokens, width), jnp.bfloat16),
        scratch_shapes=[
            pltpu.VMEM((blocks, depth, piece), jnp.bfloat16),
            pltpu.VMEM((total, depth), jnp.bfloat16),
            pltpu.VMEM((tokens, depth), jnp.bfloat16),
            pltpu.VMEM((tokens, width), jnp.bfloat16),
            pltpu.SemaphoreType.DMA((len(layout),)),
        ],
        cost_estimate=pl.CostEstimate(
            flops=2 * tokens * depth * (width + total),
            bytes_accessed=2 * (width * depth + 2 * tokens * width + total * depth),
            transcendentals=0,
        ),
        compiler_params=pltpu.CompilerParams(vmem_limit_bytes=32 * 1024 * 1024),
        name="finish_" + kind,
    )(place, vectors, inputs, main, *borders, *arrays)


def own_rows(matrix):
    across = lax.axis_size("wrow")
    rows = matrix.shape[0] // across
    return lax.dynamic_slice_in_dim(matrix, lax.axis_index("wrow") * rows, rows, 0)


def gather_single(matrix):
    along = lax.axis_size("wcol")
    piece = own_rows(matrix)
    parts = [(matrix, None, 0, None)]
    behind = [ring(piece, "wcol", by) for by in range(1, along)]
    for by, first in enumerate(behind, 1):
        held = {0: first}
        bit = lax.axis_size("wrow") // 2
        while bit:
            for k in sorted(held):
                held[k ^ bit] = swap(held[k], "wrow", bit)
            bit //= 2
        parts += [(array, None, by, k) for k, array in held.items()]
    return parts, behind


def gather_stack(stack, whole=None):
    held = {0: stack}
    bit = lax.axis_size("wrow") // 2
    while bit:
        for k in sorted(held):
            held[k ^ bit] = swap(held[k], "wrow", bit)
        bit //= 2
    start = 0 if whole is None else 1
    parts = [] if whole is None else [(whole, None, 0, None)]
    for k, array in held.items():
        for place in range(array.shape[0]):
            parts.append((array, place, place + start, k))
    return parts


def gather_plain(matrix):
    across, along = lax.axis_size("wrow"), lax.axis_size("wcol")
    leading, piece = matrix.shape
    width = piece // across
    mine = lax.dynamic_slice_in_dim(matrix, lax.axis_index("wrow") * width, width, 1)
    full = lax.all_gather(mine, ("wrow", "wcol"), axis=1, tiled=True)
    full = full.reshape(leading, across, along, width).transpose(0, 2, 1, 3)
    return full.reshape(leading, -1)


def gather_vectors(part):
    along = lax.axis_size("wcol")
    col = lax.axis_index("wcol")
    members, width = part.shape
    full = jnp.zeros((along, members, width), part.dtype)
    for by in range(along):
        piece = part if by == 0 else ring(part, "wcol", by)
        full = lax.dynamic_update_slice(full, piece[None], ((col - by) % along, 0, 0))
    return full.transpose(1, 0, 2).reshape(members, along * width)


AROUND = ((1, 0), (-1, 0), (0, 1), (0, -1), (1, 1), (1, -1), (-1, 1), (-1, -1))
BEHIND = ((1, 0), (0, 1), (1, 1))


def per_device(states, timesteps, shifts, qkv_weight, out_weight, mod_weight):
    section = lax.axis_index("section")
    across, along = lax.axis_size("wrow"), lax.axis_size("wcol")
    first = section == 0
    members, rows, cols, width = states.shape
    tokens = rows * cols
    small = across * along <= 16

    embedding = jax.nn.silu(sinusoid(timesteps, TEMB)).astype(jnp.bfloat16)
    mod_part = jnp.dot(embedding, mod_weight[0], preferred_element_type=jnp.float32).astype(
        jnp.bfloat16
    )

    if small:
        qkv_parts, _ = gather_single(qkv_weight[0])
        blocks = along
    else:
        qkv_parts = [(gather_plain(qkv_weight[0]), None, 0, None)]
        blocks = 1

    mods = gather_vectors(mod_part)
    mods_other = swap(mods, "section", 1)
    here = shifts[0]
    shifts_other = swap(here, "section", 1)
    gate_first = jnp.where(first, mods, mods_other)[:, 2 * width :].astype(jnp.float32)
    mods = mods.astype(jnp.float32)
    begin = jnp.where(first, here, shifts_other)
    turned = here - begin
    place = jnp.stack(
        [
            lax.axis_index("wrow"),
            lax.axis_index("wcol"),
            section,
            -begin[0],
            -begin[1],
            turned[0],
            turned[1],
            -here[0],
            -here[1],
        ]
    ).astype(jnp.int32)

    border = ring(states[:, :MARGIN], "wrow", -1)
    rolled = lax.dynamic_slice_in_dim(jnp.concatenate([states, border], 1), here[0], rows, 1)
    border = ring(rolled[:, :, :MARGIN], "wcol", -1)
    rolled = lax.dynamic_slice_in_dim(jnp.concatenate([rolled, border], 2), here[1], cols, 2)
    rolled = rolled.reshape(members, tokens, width)
    values = rolled.astype(jnp.float32)
    center = values - jnp.mean(values, axis=-1, keepdims=True)
    spread = jnp.mean(center * center, axis=-1, keepdims=True)
    normed = center * lax.rsqrt(spread + epsilon)
    normed = normed * (1.0 + mods[:, None, width : 2 * width]) + mods[:, None, :width]
    normed = normed.astype(jnp.bfloat16)

    if small:
        mine = own_rows(out_weight[0])
        stack = jnp.stack([mine] + [ring(mine, "wcol", by) for by in range(1, along)])
        stack = jnp.where(first, stack, swap(stack, "section", 1)), stack[1:]
        begin_parts = gather_stack(stack[0])
        own_parts = gather_stack(stack[1], out_weight[0])
    else:
        own = gather_plain(out_weight[0])
        own_parts = [(own, None, 0, None)]
        begin_parts = [(jnp.where(first, own, swap(own, "section", 1)), None, 0, None)]

    flat = states.reshape(members, tokens, width)
    results = []
    for member in range(members):
        (attended,) = attend(place, normed[member], qkv_parts, blocks, rows, cols, ())
        other = swap(attended, "section", 1)
        attended, *borders = borders_of(place, attended, other, rows, cols, AROUND)
        borders = [passed(b, *w) for b, w in zip(borders, AROUND)]
        vectors = jnp.stack(
            [gate_first[member], mods[member, width : 2 * width], mods[member, :width]]
        )
        inner = finish(
            place, vectors, rolled[member], attended, borders, begin_parts, blocks, rows, cols,
            AROUND, (5, 6), "norm",
        )
        state = finish(
            place, vectors, flat[member], attended, borders, begin_parts, blocks, rows, cols,
            AROUND, (3, 4), "state",
        )
        attended, *borders = attend(place, inner, qkv_parts, blocks, rows, cols, BEHIND)
        borders = [passed(b, *w) for b, w in zip(borders, BEHIND)]
        results.append(
            finish(
                place, mods[member, 2 * width :][None], state, attended, borders, own_parts,
                blocks, rows, cols, BEHIND, (7, 8), "last",
            )
        )
    return jnp.stack(results).reshape((1,) + states.shape)


def solution(mesh):
    in_specs = (
        P(None, "wrow", "wcol", None),
        P(),
        P("section", None),
        P("section", None, "wcol"),
        P("section", None, "wcol"),
        P("section", None, "wcol"),
    )
    out_specs = P("section", None, "wrow", "wcol", None)
    return jax.shard_map(
        per_device, mesh=mesh, in_specs=in_specs, out_specs=out_specs, check_vma=False
    )
```

```python
import functools
import math

import jax
import jax.numpy as jnp
from jax import lax
from jax.experimental import pallas as pl
from jax.experimental.pallas import tpu as pltpu
from jax.sharding import PartitionSpec as P

HEADS = 6
HD = 128
TEMB = 256
WIN = 8
MB = 2
MARGIN = WIN // 2

epsilon = 1e-06


VMEM_BLOCK = pl.BlockSpec(memory_space=pltpu.VMEM)
ANY_BLOCK = pl.BlockSpec(memory_space=pl.ANY)
SMEM_BLOCK = pl.BlockSpec(memory_space=pltpu.SMEM)


def ring(value, axis, by):
    devices = lax.axis_size(axis)
    return lax.ppermute(value, axis, [(i, (i + by) % devices) for i in range(devices)])


def swap(value, axis, bit):
    devices = lax.axis_size(axis)
    return lax.ppermute(value, axis, [(i, i ^ bit) for i in range(devices)])


def passed(value, down, right):
    across, along = lax.axis_size("wrow"), lax.axis_size("wcol")
    pairs = []
    for row in range(across):
        for col in range(along):
            target = (row + down) % across * along + (col + right) % along
            pairs.append((row * along + col, target))
    return lax.ppermute(value, ("wrow", "wcol"), pairs)


def sinusoid(moments, entries):
    half_count = entries // 2
    frequency = jnp.exp(-math.log(10000.0) * jnp.arange(half_count, dtype=jnp.float32) / half_count)
    angles = moments.astype(jnp.float32)[:, None] * frequency[None, :]
    return jnp.concatenate([jnp.cos(angles), jnp.sin(angles)], axis=1)


def copies_of(parts, refs, held, sems, row, col):
    blocks, depth, _ = held.shape
    jobs = []
    for number, (slot, index, by, k) in enumerate(parts):
        source = refs[slot]
        if index is not None:
            source = source.at[index] if len(source.shape) == 3 else source.at[pl.ds(0, index)]
        block = lax.rem(col - by + blocks, blocks) if blocks > 1 else 0
        target = held.at[block]
        if k is not None:
            rows = source.shape[0]
            start = pl.multiple_of(lax.bitwise_xor(row, k) * rows, 16)
            target = target.at[pl.ds(start, rows)]
        jobs.append((by, pltpu.make_async_copy(source, target, sems.at[number])))
    return jobs


def layout_of(parts):
    arrays, layout = [], []
    for array, index, by, k in parts:
        slot = next((i for i, a in enumerate(arrays) if a is array), None)
        if slot is None:
            slot = len(arrays)
            arrays.append(array)
        layout.append((slot, index, by, k))
    return arrays, layout


def choose(rows, cols, zones):
    matrices = []
    for top, left, high, wide in zones:
        cell = lax.broadcasted_iota(jnp.int32, (high * wide, 1), 0)
        source = (cell // wide + top) * cols + cell % wide + left
        lane = lax.broadcasted_iota(jnp.int32, (high * wide, rows * cols), 1)
        matrices.append((lane == source).astype(jnp.float32).astype(jnp.bfloat16))
    return matrices


def attend_kernel(count, layout, rows, cols, wanted, *refs):
    place, normed = refs[0], refs[1]
    parts = refs[2 : 2 + count]
    out = refs[2 + count]
    borders = refs[3 + count : 3 + count + len(wanted)]
    held, triples, sems = refs[3 + count + len(wanted) :]
    blocks, _, piece = held.shape
    width = blocks * piece // 3
    row, col = place[0], place[1]
    jobs = copies_of(layout, parts, held, sems, row, col)
    for _, job in jobs:
        job.start()
    for by in range(blocks):
        for where, job in jobs:
            if where == by:
                job.wait()
        block = lax.rem(col - by + blocks, blocks) if blocks > 1 else 0
        product = jnp.dot(normed[...], held[block], preferred_element_type=jnp.float32)
        triples[block] = product.astype(triples.dtype)

    def columns(band, start):
        got = []
        stop = start + HD
        while start < stop:
            block, inner = divmod(start, piece)
            length = min(stop - start, piece - inner)
            got.append(triples[block, band, inner : inner + length])
            start += length
        return got[0] if len(got) == 1 else jnp.concatenate(got, axis=1)

    size = WIN * cols
    side = lax.broadcasted_iota(jnp.int32, (size, size), 0) % cols // WIN
    other = lax.broadcasted_iota(jnp.int32, (size, size), 1) % cols // WIN
    same = side == other
    heads = width // HD
    for start in range(0, rows * cols, size):
        band = slice(start, start + size)
        scores = []
        for head in range(heads):
            q = columns(band, head * HD)
            k = columns(band, width + head * HD)
            scores.append(
                lax.dot_general(q, k, (((1,), (1,)), ((), ())), preferred_element_type=jnp.float32)
            )
        probabilities = []
        for score in scores:
            weights = jnp.where(same, jnp.exp(score * HD ** (-0.5)), 0.0)
            total = jnp.sum(weights, axis=-1, keepdims=True)
            probabilities.append((weights * (1.0 / total)).astype(jnp.bfloat16))
        for head in range(heads):
            v = columns(band, 2 * width + head * HD)
            attended = jnp.dot(probabilities[head], v, preferred_element_type=jnp.float32)
            out[band, head * HD : (head + 1) * HD] = attended.astype(out.dtype)
    for matrix, ref in zip(choose(rows, cols, wanted), borders):
        ref[...] = jnp.dot(matrix, out[...], preferred_element_type=jnp.float32).astype(ref.dtype)


def attend(place, normed, parts, blocks, rows, cols, wanted):
    tokens, width = normed.shape
    arrays, layout = layout_of(parts)
    piece = arrays[0].shape[-1]
    columns = blocks * piece
    inner = columns // 3
    shapes = [jax.ShapeDtypeStruct((tokens, inner), jnp.bfloat16)]
    for _, _, high, wide in wanted:
        shapes.append(jax.ShapeDtypeStruct((high * wide, inner), jnp.bfloat16))
    return pl.pallas_call(
        functools.partial(attend_kernel, len(arrays), layout, rows, cols, wanted),
        in_specs=[SMEM_BLOCK, VMEM_BLOCK] + [ANY_BLOCK] * len(arrays),
        out_specs=[VMEM_BLOCK] * len(shapes),
        out_shape=shapes,
        scratch_shapes=[
            pltpu.VMEM((blocks, width, piece), jnp.bfloat16),
            pltpu.VMEM((blocks, tokens, piece), jnp.bfloat16),
            pltpu.SemaphoreType.DMA((len(layout),)),
        ],
        cost_estimate=pl.CostEstimate(
            flops=2 * tokens * width * columns,
            bytes_accessed=2 * (width * columns + tokens * width + tokens * inner),
            transcendentals=tokens * WIN * cols * HEADS,
        ),
        compiler_params=pltpu.CompilerParams(vmem_limit_bytes=32 * 1024 * 1024),
        name="attend",
    )(place, normed, *arrays)


def side_kernel(rows, cols, zones, main, above, below, first, last, extended):
    size = above.shape[0]
    tokens = main.shape[0]
    extended[0:size] = above[...]
    extended[size : size + tokens] = main[...]
    extended[size + tokens :] = below[...]
    for matrix, ref in zip(choose(rows, cols, zones), (first, last)):
        ref[...] = jnp.dot(matrix, extended[...], preferred_element_type=jnp.float32).astype(
            ref.dtype
        )


def sides_of(main, above, below, rows, cols):
    inner = main.shape[-1]
    tall = rows + 2 * MARGIN
    shape = jax.ShapeDtypeStruct((tall * MARGIN, inner), main.dtype)
    zones = ((0, 0, tall, MARGIN), (0, cols - MARGIN, tall, MARGIN))
    return pl.pallas_call(
        functools.partial(side_kernel, tall, cols, zones),
        in_specs=[VMEM_BLOCK] * 3,
        out_specs=[VMEM_BLOCK] * 2,
        out_shape=[shape] * 2,
        scratch_shapes=[pltpu.VMEM((tall * cols, inner), main.dtype)],
        cost_estimate=pl.CostEstimate(
            flops=4 * tall * MARGIN * tall * cols * inner,
            bytes_accessed=8 * main.size,
            transcendentals=0,
        ),
        name="sides",
    )(main, above, below)


def finish_kernel(count, layout, rows, cols, wanted, shifts, kind, *refs):
    place, vectors, inputs, main = refs[:4]
    borders = refs[4 : 4 + len(wanted)]
    parts = refs[4 + len(wanted) : 4 + len(wanted) + count]
    out, held, extended, moved, result, sems = refs[4 + len(wanted) + count :]
    blocks, depth, piece = held.shape
    row, col = place[0], place[1]
    jobs = copies_of(layout, parts, held, sems, row, col)
    for _, job in jobs:
        job.start()

    tokens = rows * cols
    extended[0:tokens] = main[...]
    down, right = place[shifts[0]], place[shifts[1]]
    cell = lax.broadcasted_iota(jnp.int32, (tokens, 1), 0)
    i, j = cell // cols + down, cell % cols + right
    source = i * cols + j
    offset = tokens
    for (top, left, high, wide), ref in zip(wanted, borders):
        size = high * wide
        extended[offset : offset + size] = ref[...]
        inside = (i >= top) & (i < top + high) & (j >= left) & (j < left + wide)
        source = jnp.where(inside, offset + (i - top) * wide + (j - left), source)
        offset += size
    lane = lax.broadcasted_iota(jnp.int32, (tokens, offset), 1)
    matrix = (lane == source).astype(jnp.float32).astype(jnp.bfloat16)
    moved[...] = jnp.dot(matrix, extended[...], preferred_element_type=jnp.float32).astype(
        moved.dtype
    )
    for _, job in jobs:
        job.wait()
    for block in range(blocks):
        part = slice(block * piece, (block + 1) * piece)
        projection = jnp.dot(moved[...], held[block], preferred_element_type=jnp.float32)
        projection = projection.astype(jnp.bfloat16).astype(jnp.float32)
        state = inputs[:, part].astype(jnp.float32) + vectors[0:1, part] * projection
        result[:, part] = state.astype(result.dtype)
    if kind == "norm":
        values = result[...].astype(jnp.float32)
        center = values - jnp.mean(values, axis=-1, keepdims=True)
        spread = jnp.mean(center * center, axis=-1, keepdims=True)
        scaled = center * lax.rsqrt(spread + epsilon)
        out[...] = (scaled * (1.0 + vectors[1:2, :]) + vectors[2:3, :]).astype(out.dtype)
    elif kind == "last":
        out[...] = jnp.where(place[2] == 0, inputs[...], result[...])
    else:
        out[...] = result[...]


def finish(place, vectors, inputs, main, borders, parts, blocks, rows, cols, wanted, shifts, kind):
    tokens, width = inputs.shape
    depth = main.shape[-1]
    arrays, layout = layout_of(parts)
    piece = arrays[0].shape[-1]
    total = tokens + sum(high * wide for _, _, high, wide in wanted)
    return pl.pallas_call(
        functools.partial(finish_kernel, len(arrays), layout, rows, cols, wanted, shifts, kind),
        in_specs=[SMEM_BLOCK] + [VMEM_BLOCK] * (3 + len(wanted)) + [ANY_BLOCK] * len(arrays),
        out_specs=VMEM_BLOCK,
        out_shape=jax.ShapeDtypeStruct((tokens, width), jnp.bfloat16),
        scratch_shapes=[
            pltpu.VMEM((blocks, depth, piece), jnp.bfloat16),
            pltpu.VMEM((total, depth), jnp.bfloat16),
            pltpu.VMEM((tokens, depth), jnp.bfloat16),
            pltpu.VMEM((tokens, width), jnp.bfloat16),
            pltpu.SemaphoreType.DMA((len(layout),)),
        ],
        cost_estimate=pl.CostEstimate(
            flops=2 * tokens * depth * (width + total),
            bytes_accessed=2 * (width * depth + 2 * tokens * width + total * depth),
            transcendentals=0,
        ),
        compiler_params=pltpu.CompilerParams(vmem_limit_bytes=32 * 1024 * 1024),
        name="finish_" + kind,
    )(place, vectors, inputs, main, *borders, *arrays)


def own_rows(matrix):
    across = lax.axis_size("wrow")
    rows = matrix.shape[0] // across
    return lax.dynamic_slice_in_dim(matrix, lax.axis_index("wrow") * rows, rows, 0)


def after(value, *others):
    return lax.optimization_barrier((value,) + others)[0]


def spread(value):
    held = {0: value}
    bit = lax.axis_size("wrow") // 2
    while bit:
        for k in sorted(held):
            held[k ^ bit] = swap(held[k], "wrow", bit)
        bit //= 2
    return held


def by_distance(along):
    return sorted(range(1, along), key=lambda by: min(by, along - by))


def gather_stack(stack, whole=None):
    start = 0 if whole is None else 1
    parts = [] if whole is None else [(whole, None, 0, None)]
    for k, array in spread(stack).items():
        for place in range(array.shape[0]):
            parts.append((array, place, place + start, k))
    return parts


def gather_plain(matrix):
    across, along = lax.axis_size("wrow"), lax.axis_size("wcol")
    leading, piece = matrix.shape
    width = piece // across
    mine = lax.dynamic_slice_in_dim(matrix, lax.axis_index("wrow") * width, width, 1)
    full = lax.all_gather(mine, ("wrow", "wcol"), axis=1, tiled=True)
    full = full.reshape(leading, across, along, width).transpose(0, 2, 1, 3)
    return full.reshape(leading, -1)


def in_order(pieces):
    along = lax.axis_size("wcol")
    col = lax.axis_index("wcol")
    members, width = pieces[0].shape
    full = jnp.zeros((along, members, width), pieces[0].dtype)
    for by, piece in enumerate(pieces):
        full = lax.dynamic_update_slice(full, piece[None], ((col - by) % along, 0, 0))
    return full.transpose(1, 0, 2).reshape(members, along * width)


def per_device(states, timesteps, shifts, qkv_weight, out_weight, mod_weight):
    section = lax.axis_index("section")
    across, along = lax.axis_size("wrow"), lax.axis_size("wcol")
    first = section == 0
    members, rows, cols, width = states.shape
    tokens = rows * cols
    small = across * along <= 16
    around = (
        (-MARGIN, 0, MARGIN, cols),
        (rows, 0, MARGIN, cols),
        (-MARGIN, -MARGIN, rows + 2 * MARGIN, MARGIN),
        (-MARGIN, cols, rows + 2 * MARGIN, MARGIN),
    )
    behind = (
        (-MARGIN, 0, MARGIN, cols),
        (0, -MARGIN, rows, MARGIN),
        (-MARGIN, -MARGIN, MARGIN, MARGIN),
    )
    sent = (
        (rows - MARGIN, 0, MARGIN, cols),
        (0, cols - MARGIN, rows, MARGIN),
        (rows - MARGIN, cols - MARGIN, MARGIN, MARGIN),
    )
    ways = ((1, 0), (0, 1), (1, 1))

    embedding = jax.nn.silu(sinusoid(timesteps, TEMB)).astype(jnp.bfloat16)
    mod_part = jnp.dot(embedding, mod_weight[0], preferred_element_type=jnp.float32).astype(
        jnp.bfloat16
    )

    if small:
        matrix = qkv_weight[0]
        piece = own_rows(matrix)
        depth, columns = piece.shape
        extra = mod_part.size // columns
        carried = jnp.concatenate(
            [piece, mod_part.reshape(extra, columns), jnp.zeros((16 - extra, columns), piece.dtype)]
        )
        order = by_distance(along)
        got = {}
        for by in order:
            ready = [got[b] for b in order if min(b, along - b) < min(by, along - by)]
            got[by] = ring(after(carried, *ready) if ready else carried, "wcol", by)
        qkv_parts = [(matrix, None, 0, None)]
        for by in order:
            for k, array in spread(got[by]).items():
                qkv_parts.append((array, depth, by, k))
        blocks = along
        mods = in_order(
            [mod_part] + [got[by][depth : depth + extra].reshape(mod_part.shape) for by in range(1, along)]
        )
        done = got[order[-1]]
    else:
        full = gather_plain(qkv_weight[0])
        qkv_parts = [(full, None, 0, None)]
        blocks = 1
        mods = in_order([mod_part] + [ring(mod_part, "wcol", by) for by in range(1, along)])
        done = mods

    here = shifts[0]
    extra = jnp.zeros((1, mods.shape[1]), mods.dtype)
    extra = lax.dynamic_update_slice(extra, here[None].astype(mods.dtype), (0, 0))
    other = swap(jnp.concatenate([mods, extra]), "section", 1)
    gate_first = jnp.where(first, mods, other[:members])[:, 2 * width :].astype(jnp.float32)
    mods = mods.astype(jnp.float32)
    begin = jnp.where(first, here, other[members, :2].astype(jnp.int32))
    turned = here - begin
    place = jnp.concatenate(
        [
            jnp.stack([lax.axis_index("wrow"), lax.axis_index("wcol"), section]).astype(jnp.int32),
            -begin,
            turned,
            -here,
        ]
    )

    border = ring(states[:, :MARGIN], "wrow", -1)
    rolled = lax.dynamic_slice_in_dim(jnp.concatenate([states, border], 1), here[0], rows, 1)
    border = ring(rolled[:, :, :MARGIN], "wcol", -1)
    rolled = lax.dynamic_slice_in_dim(jnp.concatenate([rolled, border], 2), here[1], cols, 2)
    rolled = rolled.reshape(members, tokens, width)
    values = rolled.astype(jnp.float32)
    center = values - jnp.mean(values, axis=-1, keepdims=True)
    variance = jnp.mean(center * center, axis=-1, keepdims=True)
    normed = center * lax.rsqrt(variance + epsilon)
    normed = normed * (1.0 + mods[:, None, width : 2 * width]) + mods[:, None, :width]
    normed = normed.astype(jnp.bfloat16)

    if small:
        mine = after(own_rows(out_weight[0]), done)
        stack = jnp.stack([mine] + [ring(mine, "wcol", by) for by in range(1, along)])
        begin_parts = gather_stack(jnp.where(first, stack, swap(stack, "section", 1)))
        own_parts = gather_stack(stack[1:], out_weight[0])
    else:
        own = gather_plain(out_weight[0])
        own_parts = [(own, None, 0, None)]
        begin_parts = [(jnp.where(first, own, swap(own, "section", 1)), None, 0, None)]

    flat = states.reshape(members, tokens, width)
    strip = MARGIN * cols
    results = []
    for member in range(members):
        (attended,) = attend(place, normed[member], qkv_parts, blocks, rows, cols, ())
        attended = jnp.where(first, attended, swap(attended, "section", 1))
        above = ring(attended[tokens - strip :], "wrow", 1)
        below = ring(attended[:strip], "wrow", -1)
        left, right = sides_of(attended, above, below, rows, cols)
        borders = [above, below, ring(right, "wcol", 1), ring(left, "wcol", -1)]
        vectors = jnp.stack(
            [gate_first[member], mods[member, width : 2 * width], mods[member, :width]]
        )
        inner = finish(
            place, vectors, rolled[member], attended, borders, begin_parts, blocks, rows, cols,
            around, (5, 6), "norm",
        )
        state = finish(
            place, vectors, flat[member], attended, borders, begin_parts, blocks, rows, cols,
            around, (3, 4), "state",
        )
        attended, *borders = attend(place, inner, qkv_parts, blocks, rows, cols, sent)
        borders = [passed(b, *way) for b, way in zip(borders, ways)]
        results.append(
            finish(
                place, mods[member, 2 * width :][None], state, attended, borders, own_parts,
                blocks, rows, cols, behind, (7, 8), "last",
            )
        )
    return jnp.stack(results).reshape((1,) + states.shape)


def solution(mesh):
    in_specs = (
        P(None, "wrow", "wcol", None),
        P(),
        P("section", None),
        P("section", None, "wcol"),
        P("section", None, "wcol"),
        P("section", None, "wcol"),
    )
    out_specs = P("section", None, "wrow", "wcol", None)
    return jax.shard_map(
        per_device, mesh=mesh, in_specs=in_specs, out_specs=out_specs, check_vma=False
    )
```

```python
import functools
import math

import jax
import jax.numpy as jnp
from jax import lax
from jax.experimental import pallas as pl
from jax.experimental.pallas import tpu as pltpu
from jax.sharding import PartitionSpec as P


HEADS = 6
HD = 128
TEMB = 256
WIN = 8
MARGIN = WIN // 2

epsilon = 1e-06


VMEM_BLOCK = pl.BlockSpec(memory_space=pltpu.VMEM)
ANY_BLOCK = pl.BlockSpec(memory_space=pltpu.HBM)
FREE_BLOCK = pl.BlockSpec(memory_space=pl.ANY)
SMEM_BLOCK = pl.BlockSpec(memory_space=pltpu.SMEM)


def ring(value, axis, by):
    devices = lax.axis_size(axis)
    return lax.ppermute(value, axis, [(i, (i + by) % devices) for i in range(devices)])


def swap(value, axis, bit):
    devices = lax.axis_size(axis)
    return lax.ppermute(value, axis, [(i, i ^ bit) for i in range(devices)])


def passed(value, down, right):
    across, along = lax.axis_size("wrow"), lax.axis_size("wcol")
    pairs = []
    for row in range(across):
        for col in range(along):
            target = (row + down) % across * along + (col + right) % along
            pairs.append((row * along + col, target))
    return lax.ppermute(value, ("wrow", "wcol"), pairs)


def sinusoid(moments, entries):
    half_count = entries // 2
    frequency = jnp.exp(-math.log(10000.0) * jnp.arange(half_count, dtype=jnp.float32) / half_count)
    angles = moments.astype(jnp.float32)[:, None] * frequency[None, :]
    return jnp.concatenate([jnp.cos(angles), jnp.sin(angles)], axis=1)


def copies_of(parts, refs, held, sems, row, col):
    blocks, _, _ = held.shape
    jobs = []
    for number, (slot, index, by, k, offset, size) in enumerate(parts):
        source = refs[slot] if index is None else refs[slot].at[index]
        block = lax.rem(col - by + blocks, blocks) if blocks > 1 else 0
        target = held.at[block]
        if k is not None:
            rows = source.shape[0]
            start = pl.multiple_of(lax.bitwise_xor(row, k) * size + offset, 16)
            target = target.at[pl.ds(start, rows)]
        jobs.append((by, pltpu.make_async_copy(source, target, sems.at[number])))
    return jobs


def layout_of(parts):
    arrays, layout = [], []
    for array, *rest in parts:
        slot = next((i for i, a in enumerate(arrays) if a is array), None)
        if slot is None:
            slot = len(arrays)
            arrays.append(array)
        layout.append((slot, *rest))
    return arrays, layout


def choose(rows, cols, zones):
    matrices = []
    for top, left, high, wide in zones:
        cell = lax.broadcasted_iota(jnp.int32, (high * wide, 1), 0)
        source = (cell // wide + top) * cols + cell % wide + left
        lane = lax.broadcasted_iota(jnp.int32, (high * wide, rows * cols), 1)
        matrices.append((lane == source).astype(jnp.float32).astype(jnp.bfloat16))
    return matrices


def attend_kernel(count, layout, rows, cols, wanted, *refs):
    place, normed = refs[0], refs[1]
    parts = refs[2 : 2 + count]
    members = normed.shape[0]
    outs = refs[2 + count : 2 + count + members]
    start = 2 + count + members
    borders = refs[start : start + len(wanted)]
    held, triples, sems = refs[start + len(wanted) :]
    row, col = place[0], place[1]
    jobs = copies_of(layout, parts, held, sems, row, col)
    for _, job in jobs:
        job.start()
    attend_body(rows, cols, wanted, col, normed, jobs, outs, borders, held, triples)


def attend_body(rows, cols, wanted, col, normed, jobs, outs, borders, held, triples):
    members = len(outs)
    blocks, piece, _ = held.shape
    width = blocks * piece // 3
    for by in range(blocks):
        for where, job in jobs:
            if where == by:
                job.wait()
        block = lax.rem(col - by + blocks, blocks) if blocks > 1 else 0
        for member in range(members):
            product = lax.dot_general(
                held[block],
                normed[member],
                (((1,), (1,)), ((), ())),
                preferred_element_type=jnp.float32,
            )
            triples[member, block] = product.astype(triples.dtype)

    def columns(member, band, start):
        got = []
        stop = start + HD
        while start < stop:
            block, inner = divmod(start, piece)
            length = min(stop - start, piece - inner)
            got.append(triples[member, block, inner : inner + length, band])
            start += length
        return got[0] if len(got) == 1 else jnp.concatenate(got, axis=0)

    size = WIN * cols
    side = lax.broadcasted_iota(jnp.int32, (size, size), 0) % cols // WIN
    other = lax.broadcasted_iota(jnp.int32, (size, size), 1) % cols // WIN
    same = side == other
    heads = width // HD
    for member, out in enumerate(outs):
        for start in range(0, rows * cols, size):
            band = slice(start, start + size)
            scores = []
            for head in range(heads):
                q = columns(member, band, head * HD)
                k = columns(member, band, width + head * HD)
                scores.append(
                    lax.dot_general(
                        q, k, (((0,), (0,)), ((), ())), preferred_element_type=jnp.float32
                    )
                )
            probabilities = []
            for score in scores:
                weights = jnp.where(same, jnp.exp(score * HD ** (-0.5)), 0.0)
                total = jnp.sum(weights, axis=-1, keepdims=True)
                probabilities.append((weights * (1.0 / total)).astype(jnp.bfloat16))
            for head in range(heads):
                v = columns(member, band, 2 * width + head * HD)
                attended = lax.dot_general(
                    probabilities[head],
                    v,
                    (((1,), (1,)), ((), ())),
                    preferred_element_type=jnp.float32,
                )
                out[band, head * HD : (head + 1) * HD] = attended.astype(out.dtype)
        for matrix, ref in zip(choose(rows, cols, wanted), borders):
            cells = jnp.dot(matrix, out[...], preferred_element_type=jnp.float32)
            ref[member] = cells.astype(ref.dtype)


def attend(place, normed, parts, blocks, rows, cols, wanted):
    members, tokens, width = normed.shape
    arrays, layout = layout_of(parts)
    piece = arrays[0].shape[0]
    columns = blocks * piece
    inner = columns // 3
    shapes = [jax.ShapeDtypeStruct((tokens, inner), jnp.bfloat16)] * members
    for _, _, high, wide in wanted:
        shapes.append(jax.ShapeDtypeStruct((members, high * wide, inner), jnp.bfloat16))
    got = pl.pallas_call(
        functools.partial(attend_kernel, len(arrays), layout, rows, cols, wanted),
        in_specs=[SMEM_BLOCK, VMEM_BLOCK] + [ANY_BLOCK] * len(arrays),
        out_specs=[VMEM_BLOCK] * len(shapes),
        out_shape=shapes,
        scratch_shapes=[
            pltpu.VMEM((blocks, piece, width), jnp.bfloat16),
            pltpu.VMEM((members, blocks, piece, tokens), jnp.bfloat16),
            pltpu.SemaphoreType.DMA((len(layout),)),
        ],
        cost_estimate=pl.CostEstimate(
            flops=2 * members * tokens * width * columns,
            bytes_accessed=2 * (width * columns + members * tokens * (width + inner)),
            transcendentals=members * tokens * WIN * cols * HEADS,
        ),
        compiler_params=pltpu.CompilerParams(vmem_limit_bytes=56 * 1024 * 1024),
        name="attend",
    )(place, normed, *arrays)
    return got[:members], got[members:]


def side_kernel(rows, cols, zones, place, mine, theirs, above, below, main, first, last, extended):
    size = above.shape[0]
    tokens = main.shape[0]
    main[...] = jnp.where(place[2] == 0, mine[...], theirs[...])
    extended[0:size] = above[...]
    extended[size : size + tokens] = main[...]
    extended[size + tokens :] = below[...]
    for matrix, ref in zip(choose(rows, cols, zones), (first, last)):
        ref[...] = jnp.dot(matrix, extended[...], preferred_element_type=jnp.float32).astype(
            ref.dtype
        )


def sides_of(place, main, theirs, above, below, rows, cols):
    inner = main.shape[-1]
    tall = rows + 2 * MARGIN
    shape = jax.ShapeDtypeStruct((tall * MARGIN, inner), main.dtype)
    zones = ((0, 0, tall, MARGIN), (0, cols - MARGIN, tall, MARGIN))
    return pl.pallas_call(
        functools.partial(side_kernel, tall, cols, zones),
        in_specs=[SMEM_BLOCK] + [VMEM_BLOCK] * 4,
        out_specs=[VMEM_BLOCK] * 3,
        out_shape=[jax.ShapeDtypeStruct(main.shape, main.dtype), shape, shape],
        scratch_shapes=[pltpu.VMEM((tall * cols, inner), main.dtype)],
        cost_estimate=pl.CostEstimate(
            flops=4 * tall * MARGIN * tall * cols * inner,
            bytes_accessed=8 * main.size,
            transcendentals=0,
        ),
        name="sides",
    )(place, main, theirs, above, below)


def moving(rows, cols, down, right, zones):
    tokens = rows * cols
    cell = lax.broadcasted_iota(jnp.int32, (tokens, 1), 0)
    i, j = cell // cols + down, cell % cols + right
    source = i * cols + j
    offset = tokens
    for top, left, high, wide in zones:
        inside = (i >= top) & (i < top + high) & (j >= left) & (j < left + wide)
        source = jnp.where(inside, offset + (i - top) * wide + (j - left), source)
        offset += high * wide
    lane = lax.broadcasted_iota(jnp.int32, (tokens, offset), 1)
    return (lane == source).astype(jnp.float32).astype(jnp.bfloat16)


def normalized(values, shift, scale):
    center = values - jnp.mean(values, axis=-1, keepdims=True)
    variance = jnp.mean(center * center, axis=-1, keepdims=True)
    return center * lax.rsqrt(variance + epsilon) * (1.0 + scale) + shift


def prepare_kernel(count, rows, cols, zones, place, states, mine, theirs, edge, *refs):
    members, tokens, width = states.shape
    pieces, mods = refs[:count], refs[count]
    rolled, normed, extended, held = refs[count + 1 :]
    piece = pieces[0].shape[-1]
    for by, ref in enumerate(pieces):
        held[lax.rem(place[1] - by + count, count)] = ref[...].astype(jnp.float32)
    for block in range(count):
        mods[:, block * piece : (block + 1) * piece] = held[block]
    matrix = moving(rows, cols, -place[7], -place[8], zones)
    side = mine.shape[0]
    for member in range(members):
        extended[0:tokens] = states[member]
        extended[tokens : tokens + side] = jnp.where(place[2] == member, mine[...], theirs[...])
        extended[tokens + side :] = edge[member]
        moved = jnp.dot(matrix, extended[...], preferred_element_type=jnp.float32)
        rolled[member] = moved.astype(rolled.dtype)
        shift = mods[member : member + 1, 0:width]
        scale = mods[member : member + 1, width : 2 * width]
        normed[member] = normalized(moved, shift, scale).astype(normed.dtype)


def prepare(place, states, mine, theirs, edge, pieces, rows, cols):
    members, tokens, width = states.shape
    zones = ((0, cols, rows, MARGIN), (rows, 0, MARGIN, cols), (rows, cols, MARGIN, MARGIN))
    total = tokens + sum(high * wide for _, _, high, wide in zones)
    count, piece = len(pieces), pieces[0].shape[-1]
    shape = jax.ShapeDtypeStruct(states.shape, states.dtype)
    return pl.pallas_call(
        functools.partial(prepare_kernel, count, rows, cols, zones),
        in_specs=[SMEM_BLOCK] + [VMEM_BLOCK] * (4 + count),
        out_specs=[VMEM_BLOCK] * 3,
        out_shape=[jax.ShapeDtypeStruct((members, count * piece), jnp.float32), shape, shape],
        scratch_shapes=[
            pltpu.VMEM((total, width), states.dtype),
            pltpu.VMEM((count, members, piece), jnp.float32),
        ],
        cost_estimate=pl.CostEstimate(
            flops=2 * members * tokens * total * width,
            bytes_accessed=8 * members * tokens * width,
            transcendentals=0,
        ),
        compiler_params=pltpu.CompilerParams(vmem_limit_bytes=56 * 1024 * 1024),
        name="prepare",
    )(place, states, mine, theirs, edge, *pieces)


def finish_kernel(members, slots, count, layout, rows, cols, wanted, shifts, kind, *refs):
    place = refs[0]
    mods, others = refs[1], refs[2]
    groups = [[refs[3 + slot] for slot in group] for group in slots]
    start = 4 + max(slot for group in slots for slot in group)
    parts = refs[start : start + count]
    out, held, extended, moved, result, sems = refs[start + count :]
    jobs = copies_of(layout, parts, held, sems, place[0], place[1])
    for _, job in jobs:
        job.start()
    scratch = held, extended, moved, result
    finish_body(members, rows, cols, wanted, shifts, kind, place, mods, others, groups, jobs, out, scratch)


def finish_body(
    members, rows, cols, wanted, shifts, kind, place, mods, others, groups, jobs, out, scratch
):
    held, extended, moved, result = scratch
    blocks, _, piece = held.shape
    tokens = rows * cols
    width = out.shape[-1]
    matrix = moving(rows, cols, place[shifts[0]], place[shifts[1]], wanted)
    for member, (_, main, *borders) in enumerate(groups):
        extended[0:tokens] = main[...]
        offset = tokens
        for ref in borders:
            size = ref.shape[-2]
            cells = ref[...] if len(ref.shape) == 2 else ref[members[member]]
            extended[offset : offset + size] = cells
            offset += size
        moved[member] = jnp.dot(
            matrix, extended[...], preferred_element_type=jnp.float32
        ).astype(moved.dtype)
    for _, job in jobs:
        job.wait()
    for member, (inputs, *_) in enumerate(groups):
        who = slice(members[member], members[member] + 1)
        gate = mods[who, 2 * width :]
        if kind != "last":
            gate = jnp.where(place[2] == 0, gate, others[who, 2 * width :])
        for block in range(blocks):
            part = slice(block * piece, (block + 1) * piece)
            projection = jnp.dot(moved[member], held[block], preferred_element_type=jnp.float32)
            projection = projection.astype(jnp.bfloat16).astype(jnp.float32)
            residual = inputs[:, part] if len(inputs.shape) == 2 else inputs[members[member], :, part]
            state = residual.astype(jnp.float32) + gate[:, part] * projection
            state = state.astype(out.dtype)
            if kind == "norm":
                result[:, part] = state
            elif kind == "last":
                out[member, :, part] = jnp.where(place[2] == 0, residual, state)
            else:
                out[member, :, part] = state
        if kind == "norm":
            shift, scale = mods[who, 0:width], mods[who, width : 2 * width]
            values = result[...].astype(jnp.float32)
            out[member] = normalized(values, shift, scale).astype(out.dtype)


def operands_of(groups):
    operands, slots = [], []
    for _, inputs, main, borders in groups:
        slots.append([])
        for array in (inputs, main, *borders):
            slot = next((i for i, a in enumerate(operands) if a is array), len(operands))
            operands += [array] if slot == len(operands) else []
            slots[-1].append(slot)
    return operands, slots


def advance_kernel(members, slots, counts, layouts, rows, cols, wanted, shifts, sent, *refs):
    place, mods, others = refs[:3]
    groups = [[refs[3 + slot] for slot in group] for group in slots]
    start = 4 + max(slot for group in slots for slot in group)
    first_parts = refs[start : start + counts[0]]
    start += counts[0]
    second_parts = refs[start : start + counts[1]]
    start += counts[1]
    outs = refs[start : start + len(members)]
    start += len(members)
    borders = refs[start : start + len(sent)]
    held, extended, moved, result, normed, weight, triples, sems, more = refs[start + len(sent) :]
    row, col = place[0], place[1]
    jobs = copies_of(layouts[0], first_parts, held, sems, row, col)
    later = copies_of(layouts[1], second_parts, weight, more, row, col)
    for _, job in jobs + later:
        job.start()
    scratch = held, extended, moved, result
    finish_body(
        members, rows, cols, wanted, shifts, "norm", place, mods, others, groups, jobs, normed, scratch
    )
    attend_body(rows, cols, sent, col, normed, later, outs, borders, weight, triples)


def advance(place, mods, others, groups, out_parts, qkv_parts, blocks, rows, cols, wanted, shifts, sent):
    numbers = tuple(group[0] for group in groups)
    members = len(groups)
    tokens, width = groups[0][1].shape[-2:]
    depth = groups[0][2].shape[-1]
    operands, slots = operands_of(groups)
    first, first_layout = layout_of(out_parts)
    second, second_layout = layout_of(qkv_parts)
    piece, columns = first[0].shape[-1], second[0].shape[0]
    total = tokens + sum(high * wide for _, _, high, wide in wanted)
    shapes = [jax.ShapeDtypeStruct((tokens, depth), jnp.bfloat16)] * members
    for _, _, high, wide in sent:
        shapes.append(jax.ShapeDtypeStruct((members, high * wide, depth), jnp.bfloat16))
    got = pl.pallas_call(
        functools.partial(
            advance_kernel,
            numbers,
            slots,
            (len(first), len(second)),
            (first_layout, second_layout),
            rows,
            cols,
            wanted,
            shifts,
            sent,
        ),
        in_specs=[SMEM_BLOCK]
        + [VMEM_BLOCK] * (2 + len(operands))
        + [FREE_BLOCK] * len(first)
        + [ANY_BLOCK] * len(second),
        out_specs=[VMEM_BLOCK] * len(shapes),
        out_shape=shapes,
        scratch_shapes=[
            pltpu.VMEM((blocks, depth, piece), jnp.bfloat16),
            pltpu.VMEM((total, depth), jnp.bfloat16),
            pltpu.VMEM((members, tokens, depth), jnp.bfloat16),
            pltpu.VMEM((tokens, width), jnp.bfloat16),
            pltpu.VMEM((members, tokens, width), jnp.bfloat16),
            pltpu.VMEM((blocks, columns, width), jnp.bfloat16),
            pltpu.VMEM((members, blocks, columns, tokens), jnp.bfloat16),
            pltpu.SemaphoreType.DMA((len(first_layout),)),
            pltpu.SemaphoreType.DMA((len(second_layout),)),
        ],
        cost_estimate=pl.CostEstimate(
            flops=2 * members * tokens * (depth * (width + total) + width * columns * blocks),
            bytes_accessed=2 * width * (depth + columns * blocks + members * tokens),
            transcendentals=members * tokens * WIN * cols * HEADS,
        ),
        compiler_params=pltpu.CompilerParams(vmem_limit_bytes=56 * 1024 * 1024),
        name="advance",
    )(place, mods, others, *operands, *first, *second)
    return got[:members], got[members:]


def finish(place, mods, others, groups, parts, blocks, rows, cols, wanted, shifts, kind):
    numbers = tuple(group[0] for group in groups)
    members = len(groups)
    tokens, width = groups[0][1].shape[-2:]
    depth = groups[0][2].shape[-1]
    arrays, layout = layout_of(parts)
    piece = arrays[0].shape[-1]
    total = tokens + sum(high * wide for _, _, high, wide in wanted)
    operands, slots = operands_of(groups)
    operands = [mods, others] + operands
    return pl.pallas_call(
        functools.partial(
            finish_kernel, numbers, slots, len(arrays), layout, rows, cols, wanted, shifts, kind
        ),
        in_specs=[SMEM_BLOCK] + [VMEM_BLOCK] * len(operands) + [FREE_BLOCK] * len(arrays),
        out_specs=VMEM_BLOCK,
        out_shape=jax.ShapeDtypeStruct((members, tokens, width), jnp.bfloat16),
        scratch_shapes=[
            pltpu.VMEM((blocks, depth, piece), jnp.bfloat16),
            pltpu.VMEM((total, depth), jnp.bfloat16),
            pltpu.VMEM((members, tokens, depth), jnp.bfloat16),
            pltpu.VMEM((tokens, width), jnp.bfloat16),
            pltpu.SemaphoreType.DMA((len(layout),)),
        ],
        cost_estimate=pl.CostEstimate(
            flops=2 * members * tokens * depth * (width + total),
            bytes_accessed=2 * (width * depth + members * (2 * tokens * width + total * depth)),
            transcendentals=0,
        ),
        compiler_params=pltpu.CompilerParams(vmem_limit_bytes=56 * 1024 * 1024),
    )(place, *operands, *arrays)


def own_rows(matrix):
    across = lax.axis_size("wrow")
    rows = matrix.shape[0] // across
    return lax.dynamic_slice_in_dim(matrix, lax.axis_index("wrow") * rows, rows, 0)


def after(value, *others):
    return lax.optimization_barrier((value,) + others)[0]


def spread(value):
    held = {0: value}
    bit = lax.axis_size("wrow") // 2
    while bit:
        for k in sorted(held):
            held[k ^ bit] = swap(held[k], "wrow", bit)
        bit //= 2
    return held


def half_of(size):
    return -(-size // 32) * 16


def by_distance(along):
    return sorted(range(1, along), key=lambda by: min(by, along - by))


def gather_stack(stack, whole=None):
    start = 0 if whole is None else 1
    parts = [] if whole is None else [(whole, None, 0, None, 0, 1)]
    for k, array in spread(stack).items():
        for place in range(array.shape[0]):
            parts.append((array, place, place + start, k, 0, array.shape[1]))
    return parts


def gather_plain(matrix):
    across, along = lax.axis_size("wrow"), lax.axis_size("wcol")
    leading, piece = matrix.shape
    width = piece // across
    mine = lax.dynamic_slice_in_dim(matrix, lax.axis_index("wrow") * width, width, 1)
    full = lax.all_gather(mine, ("wrow", "wcol"), axis=1, tiled=True)
    full = full.reshape(leading, across, along, width).transpose(0, 2, 1, 3)
    return full.reshape(leading, -1)


def per_device(states, timesteps, shifts, qkv_weight, out_weight, mod_weight):
    section = lax.axis_index("section")
    across, along = lax.axis_size("wrow"), lax.axis_size("wcol")
    first = section == 0
    members, rows, cols, width = states.shape
    tokens = rows * cols
    small = across * along <= 16
    around = (
        (-MARGIN, 0, MARGIN, cols),
        (rows, 0, MARGIN, cols),
        (-MARGIN, -MARGIN, rows + 2 * MARGIN, MARGIN),
        (-MARGIN, cols, rows + 2 * MARGIN, MARGIN),
    )
    behind = (
        (-MARGIN, 0, MARGIN, cols),
        (0, -MARGIN, rows, MARGIN),
        (-MARGIN, -MARGIN, MARGIN, MARGIN),
    )
    sent = (
        (rows - MARGIN, 0, MARGIN, cols),
        (0, cols - MARGIN, rows, MARGIN),
        (rows - MARGIN, cols - MARGIN, MARGIN, MARGIN),
    )
    ways = ((1, 0), (0, 1), (1, 1))

    embedding = jax.nn.silu(sinusoid(timesteps, TEMB)).astype(jnp.bfloat16)
    mod_part = jnp.dot(embedding, mod_weight[0], preferred_element_type=jnp.float32).astype(
        jnp.bfloat16
    )

    if small:
        matrix = qkv_weight[0].T
        piece = own_rows(matrix)
        size = piece.shape[0]
        half = half_of(size)
        got = {}
        for by in by_distance(along):
            if by in (1, along - 1):
                chunks = [(0, piece)]
            else:
                chunks = [(0, piece[:half]), (half, piece[half:])]
            for offset, chunk in chunks:
                got[by, offset] = ring(chunk, "wcol", by)
        qkv_parts = [(matrix, None, 0, None, 0, 1)]
        for (by, offset), chunk in got.items():
            for k, array in spread(chunk).items():
                qkv_parts.append((array, None, by, k, offset, size))
        blocks = along
        pieces = [mod_part]
        for by in range(1, along):
            pieces.append(ring(mod_part, "wcol", by))
    else:
        full = gather_plain(qkv_weight[0]).T
        qkv_parts = [(full, None, 0, None, 0, 1)]
        blocks = 1
        pieces = [mod_part] + [ring(mod_part, "wcol", by) for by in range(1, along)]

    here = shifts[0]
    begin_shift = jnp.where(first, here, swap(here, "section", 1))
    place = jnp.concatenate(
        [
            jnp.stack([lax.axis_index("wrow"), lax.axis_index("wcol"), section]).astype(jnp.int32),
            -begin_shift,
            here - begin_shift,
            -here,
        ]
    )

    side = states[:, :, :MARGIN].reshape(members, rows * MARGIN, width)
    side = lax.dynamic_index_in_dim(side, section, 0, keepdims=False)
    side_mine = ring(side, "wcol", -1)
    side_theirs = swap(side_mine, "section", 1)
    top = (side_mine[: MARGIN * MARGIN], side_theirs[: MARGIN * MARGIN])
    corner = jnp.where(first, jnp.stack(top), jnp.stack(top[::-1]))
    flat = states.reshape(members, tokens, width)
    edge = jnp.concatenate([flat[:, : MARGIN * cols], corner], axis=1)
    edge = ring(edge, "wrow", -1)
    mods, rolled, normed = prepare(
        place, flat, side_mine, side_theirs, edge, pieces, rows, cols
    )
    others = swap(mods, "section", 1)

    if small:
        mine = own_rows(out_weight[0])
        theirs = swap(mine, "section", 1)
        late = qkv_parts[-2][0]
        begin = [jnp.where(first, mine, theirs)]
        own = []
        for by in range(1, along):
            begin.append(after(ring(begin[0], "wcol", by), late))
            own.append(ring(mine, "wcol", by))
        begin_parts = gather_stack(jnp.stack(begin))
    else:
        own = gather_plain(out_weight[0])
        own_parts = [(own, None, 0, None, 0, 1)]
        begin_parts = [(jnp.where(first, own, swap(own, "section", 1)), None, 0, None, 0, 1)]

    strip = MARGIN * cols
    moved, gate = [], ()
    values, _ = attend(place, normed, qkv_parts, blocks, rows, cols, ())
    others_values = []
    for member in range(members):
        others_values.append(swap(values[member], "section", 1))
    for member in range(members):
        mine, theirs = values[member], after(others_values[member], *gate)
        last = jnp.where(first, mine[tokens - strip :], theirs[tokens - strip :])
        above = ring(last, "wrow", 1)
        below = ring(jnp.where(first, mine[:strip], theirs[:strip]), "wrow", -1)
        attended, left, right = sides_of(place, mine, theirs, above, below, rows, cols)
        borders = [above, below, ring(right, "wcol", 1), ring(left, "wcol", -1)]
        moved.append((attended, borders))
        gate = (left,)
    if small:
        own = jnp.stack([after(piece, left) for piece in own])
        own_parts = gather_stack(own, out_weight[0])
    values, borders = advance(
        place, mods, others, [(m, rolled, *moved[m]) for m in range(members)],
        begin_parts, qkv_parts, blocks, rows, cols, around, (5, 6), sent,
    )
    states_now = finish(
        place, mods, others, [(m, flat, *moved[m]) for m in range(members)],
        begin_parts, blocks, rows, cols, around, (3, 4), "state",
    )
    borders = [passed(border, *way) for border, way in zip(borders, ways)]
    groups = [(m, states_now, values[m], borders) for m in range(members)]
    result = finish(
        place, mods, others, groups, own_parts, blocks, rows, cols, behind, (7, 8), "last"
    )
    return result.reshape((1,) + states.shape)


def solution(mesh):
    in_specs = (
        P(None, "wrow", "wcol", None),
        P(),
        P("section", None),
        P("section", None, "wcol"),
        P("section", None, "wcol"),
        P("section", None, "wcol"),
    )
    out_specs = P("section", None, "wrow", "wcol", None)

    return jax.shard_map(
        per_device, mesh=mesh, in_specs=in_specs, out_specs=out_specs, check_vma=False
    )
```
